256 devices in a mesh: segment: 4 (over x), space: 64 (over z, y, core).
Axes of the slice: x: 4, y: 4, z: 8, core: 2. Of those that a mesh axis runs over, the one named last changes fastest.
Arguments:
- frames: bfloat16 [4, 1024, 32, 64], P(None, 'space'), may hold values from -6 to 6
- hidden_prev: bfloat16 [4, 4, 1024, 32, 128], P('segment', None, 'space'), may hold values from -1 to 1
- cell_prev: float32 [4, 4, 1024, 32, 128], P('segment', None, 'space'), may hold values from -6 to 6
- kernels: bfloat16 [4, 5, 5, 256, 512], P('segment'), may hold values from -0.078125 to 0.078125
- biases: float32 [4, 512], P('segment'), may hold values from -4 to 4
Outputs:
- hidden_next: bfloat16 [4, 4, 1024, 32, 128], P('segment', None, 'space')
- cell_next: float32 [4, 4, 1024, 32, 128], P('segment', None, 'space')
The draws below stay inside these ranges and needn't reach their ends.
All inputs are finite; a program needn't handle non-finite values.
Results may differ from the reference program's by a relative error of at most 0.0095.
Values may be sent and summed in bfloat16 or wider, within the bound.
A program may use at most 128 MiB of HBM per device.

```python
import jax
import jax.numpy as jnp

NARROW = 64
WIDE = 128
KER = 5
MICRO = 4
COLS = 32
LAYERS = 4
ROWS = 1024


def steps_of(key, shape, split, low, largest):
    factor_of, own = 1.0, jax.random.fold_in(key, 6)
    for dim, shards_of in split:
        steps = jnp.exp(jax.random.uniform(jax.random.fold_in(own, dim), (shards_of,), jnp.float32, low / len(split), largest / len(split)))
        factor_of = factor_of * jnp.repeat(steps, shape[dim] // shards_of).reshape([-1 if axis == dim else 1 for axis in range(len(shape))])
    return factor_of


def gaussian(stream_key, shape, scale, reach, pieces=(), held_as=jnp.bfloat16):
    drawn = jax.random.normal(stream_key, shape, jnp.float32) * scale
    if len(pieces) > 0:
        drawn = steps_of(stream_key, shape, pieces, -0.22, 0.18) * drawn
    return jnp.clip(drawn, min=-reach, max=reach).astype(held_as)


def setup_inputs(seed: int = 0) -> dict:
    keys = jax.random.split(jax.random.key(seed), 6)
    frames = gaussian(keys[0], (MICRO, ROWS, COLS, NARROW), 1.0, 6.0, ((1, 64),))
    hidden_prev = jnp.clip(jax.random.uniform(keys[1], (LAYERS, MICRO, ROWS, COLS, WIDE), jnp.float32, -1.0, 1.0) * steps_of(keys[1], (LAYERS, MICRO, ROWS, COLS, WIDE), ((0, 4), (2, 64)), -0.4, 0.0), -1.0, 1.0).astype(jnp.bfloat16)
    cell_prev = gaussian(keys[2], (LAYERS, MICRO, ROWS, COLS, WIDE), 1.0, 6.0, ((0, 4), (2, 64)), jnp.float32)
    kernels = gaussian(keys[3], (LAYERS, KER, KER, 2 * WIDE, 4 * WIDE), (KER * KER * 2 * WIDE) ** -0.5, 0.078125, ((0, 4),))
    biases = gaussian(keys[4], (LAYERS, 4 * WIDE), 1.0, 4.0, ((0, 4),), jnp.float32)
    return {"frames": frames, "hidden_prev": hidden_prev, "cell_prev": cell_prev, "kernels": kernels, "biases": biases}


def layer_kernel(kernel, inputs_width, hidden_width, wide):
    rows_cut = jnp.concatenate([kernel[:, :, 0:inputs_width], kernel[:, :, wide:wide + hidden_width]], axis=2)
    return jnp.concatenate([rows_cut[..., k * wide:k * wide + hidden_width] for k in range(4)], axis=-1)


def layer_bias(bias, hidden_width, wide):
    return jnp.concatenate([bias[k * wide:k * wide + hidden_width] for k in range(4)], axis=-1)


def conv_gates(joined, kernel, bias):
    rows = joined.shape[0]
    cols = joined.shape[1]
    padded = jnp.pad(joined, ((2, 2), (2, 2), (0, 0)))
    total = jnp.zeros((rows * cols, kernel.shape[-1]), jnp.float32)
    for first in range(5):
        for second in range(5):
            window = padded[first:first + rows, second:second + cols, :].reshape(rows * cols, -1)
            total = total + jnp.dot(window, kernel[first, second], preferred_element_type=jnp.float32)
    return (total + bias).reshape(rows, cols, -1)


def reference(frames, hidden_prev, cell_prev, kernels, biases):
    wide = hidden_prev.shape[-1]
    narrow = frames.shape[-1]
    hidden_widths = [narrow, wide, wide, narrow]
    input_widths = [narrow, narrow, wide, wide]
    hidden_all = []
    cell_all = []
    inputs = frames
    for layer in range(LAYERS):
        hid = hidden_widths[layer]
        cin = input_widths[layer]
        kernel = layer_kernel(kernels[layer], cin, hid, wide)
        bias = layer_bias(biases[layer], hid, wide)
        hidden_layer = []
        cell_layer = []
        for batch in range(MICRO):
            joined = jnp.concatenate([inputs[batch][..., 0:cin], hidden_prev[layer, batch][..., 0:hid]], axis=-1)
            gates = conv_gates(joined, kernel, bias)
            gate_in = jax.nn.sigmoid(gates[..., 0:hid])
            gate_forget = jax.nn.sigmoid(gates[..., hid:2 * hid])
            candidate = jnp.tanh(gates[..., 2 * hid:3 * hid])
            gate_out = jax.nn.sigmoid(gates[..., 3 * hid:4 * hid])
            cell_new = gate_forget * cell_prev[layer, batch][..., 0:hid] + gate_in * candidate
            hidden_new = (gate_out * jnp.tanh(cell_new)).astype(jnp.bfloat16)
            widen = ((0, 0), (0, 0), (0, wide - hid))
            hidden_layer.append(jnp.pad(hidden_new, widen))
            cell_layer.append(jnp.pad(cell_new, widen))
        inputs = jnp.stack(hidden_layer)
        hidden_all.append(inputs)
        cell_all.append(jnp.stack(cell_layer))
    return jnp.stack(hidden_all), jnp.stack(cell_all)
```

```python
import functools

import jax
import jax.numpy as jnp
from jax import lax
from jax.experimental import pallas as pl
from jax.experimental.pallas import tpu as pltpu
from jax.sharding import PartitionSpec as P

MESH = pl.DeviceIdType.MESH
F32 = jnp.float32
BF16 = jnp.bfloat16
KER = 5
HALO = 2


def lane_halves(low, high):
    lane = lax.broadcasted_iota(jnp.int32, low.shape, low.ndim - 1)
    return jnp.where(lane < 64, low, pltpu.roll(high, 64, low.ndim - 1))


def put_shifts(value, dst):
    rows, cols, chans = value.shape
    flat = value.reshape(rows * cols, chans)
    col = lax.broadcasted_iota(jnp.int32, (rows, cols, chans), 1).reshape(rows * cols, chans)
    for b in range(KER):
        by = b - HALO
        if by == 0:
            moved = flat
        else:
            moved = pltpu.roll(flat, (-by) % (rows * cols), 0)
            inside = (col < cols - by) if by > 0 else (col >= -by)
            moved = jnp.where(inside, moved, 0.0)
        dst[:, :, 128 * b : 128 * (b + 1)] = moved.astype(BF16).reshape(rows, cols, chans)


def conv(buf, weights, rows, cols, step, first=0, count=None):
    taps = weights.shape[0]
    lhs = jnp.concatenate(
        [buf[step * a : step * a + rows].reshape(rows * cols, KER * 128) for a in range(taps)], axis=1
    )
    n = weights.shape[-1]
    return jnp.dot(lhs, weights[...].reshape(taps * KER * 128, n), preferred_element_type=F32)


def sigmoid(x):
    return 0.5 * jnp.tanh(0.5 * x) + 0.5


def kernel(
    segments, spaces,
    frames, hprev, cprev, kern, bias_in,
    hout, cout,
    wx, wh, w3, wxc, w3c, bias, biasc,
    fraw, hraw, xraw, shift_a, shift_b, acc, cell, cnew, hnew,
    w_sem, in_sem, halo_send, halo_recv, x_send, x_recv, out_sem,
):
    seg = lax.axis_index("segment")
    sp = lax.axis_index("space")
    batches, rows, cols = (frames.shape[0], frames.shape[1], frames.shape[2])
    m_rows = rows * cols
    top, bottom = (sp > 0, sp < spaces - 1)
    above, below = (lax.rem(sp + spaces - 1, spaces), lax.rem(sp + 1, spaces))
    nxt, prv = (lax.rem(seg + 1, segments), lax.rem(seg + segments - 1, segments))

    barrier = pltpu.get_barrier_semaphore()
    others = [(seg, above), (seg, below)]
    others += [(k, s) for k in (nxt, prv) for s in (above, sp, below)]
    for other in others:
        pl.semaphore_signal(barrier, inc=1, device_id=other, device_id_type=MESH)

    def remote(src, dst, send, recv, k, s):
        return pltpu.make_async_remote_copy(
            src_ref=src, dst_ref=dst, send_sem=send, recv_sem=recv, device_id=(k, s), device_id_type=MESH
        )

    def local(src, dst, sem):
        return pltpu.make_async_copy(src, dst, sem)

    def weight_copies(layer):
        if layer == 0:
            for a in range(KER):
                yield local(kern.at[0, a, :, 0:64], wx.at[a, :, 0:64], w_sem.at[a])
                yield local(kern.at[0, a, :, 128:192], wx.at[a, :, 64:128], w_sem.at[KER + a])
        elif layer == 1:
            for a in range(KER):
                yield local(kern.at[0, a, :, 128:256], wh.at[a], w_sem.at[a])
            for a in range(KER):
                half = 64 * (a % 2)
                yield local(kern.at[0, a, :, 0:64], w3.at[a // 2, :, half : half + 64], w_sem.at[KER + a])
        elif layer == 2:
            for a in range(KER):
                yield local(kern.at[0, a, :, 128:256], wh.at[a], w_sem.at[a])
            for a in range(KER):
                yield local(kern.at[0, a, :, 0:128], wx.at[a], w_sem.at[KER + a])
        else:
            for a in range(KER):
                half = 64 * (a % 2)
                yield local(kern.at[0, a, :, 128:192], w3.at[a // 2, :, half : half + 64], w_sem.at[a])
            for a in range(KER):
                yield local(kern.at[0, a, :, 0:128], wx.at[a], w_sem.at[KER + a])

    state_in = [
        local(hprev.at[0], hraw.at[:, HALO : HALO + rows], in_sem.at[0]),
        local(bias_in, bias, in_sem.at[1]),
        local(cprev.at[0], cell, in_sem.at[2]),
    ]
    frames_in = local(frames, fraw.at[:, HALO : HALO + rows], in_sem.at[3])
    state_in[0].start()
    pl.when(seg == 0)(frames_in.start)
    for layer in range(4):

        @pl.when(seg == layer)
        def _(layer=layer):
            for copy in weight_copies(layer):
                copy.start()

    state_in[1].start()
    state_in[2].start()

    def edges(src, dst, index):
        up = remote(src.at[:, 0:HALO], dst.at[:, HALO + rows :], halo_send.at[index], halo_recv.at[index], seg, above)
        down = remote(
            src.at[:, rows - HALO :], dst.at[:, 0:HALO], halo_send.at[index + 1], halo_recv.at[index + 1], seg, below
        )
        return (up, down)

    pl.semaphore_wait(barrier, len(others))
    h_up, h_down = edges(hprev.at[0], hraw, 0)
    f_up, f_down = edges(frames, fraw, 2)
    pl.when(top)(h_up.start)
    pl.when(bottom)(h_down.start)
    pl.when(jnp.logical_and(seg == 0, top))(f_up.start)
    pl.when(jnp.logical_and(seg == 0, bottom))(f_down.start)

    @pl.when(sp == 0)
    def _():
        hraw[:, 0:HALO] = jnp.zeros((batches, HALO, cols, 128), BF16)
        xraw[:, 0:HALO] = jnp.zeros((batches, HALO, cols, 128), BF16)
        fraw[:, 0:HALO] = jnp.zeros((batches, HALO, cols, 64), BF16)

    @pl.when(sp == spaces - 1)
    def _():
        hraw[:, HALO + rows :] = jnp.zeros((batches, HALO, cols, 128), BF16)
        xraw[:, HALO + rows :] = jnp.zeros((batches, HALO, cols, 128), BF16)
        fraw[:, HALO + rows :] = jnp.zeros((batches, HALO, cols, 64), BF16)

    def sends(m):
        return (
            remote(hnew.at[m], xraw.at[m, HALO : HALO + rows], x_send.at[m, 0], x_recv.at[m, 0], nxt, sp),
            remote(
                hnew.at[m, 0:HALO], xraw.at[m, HALO + rows :], x_send.at[m, 1], x_recv.at[m, 1], nxt, above
            ),
            remote(
                hnew.at[m, rows - HALO :], xraw.at[m, 0:HALO], x_send.at[m, 2], x_recv.at[m, 2], nxt, below
            ),
        )

    def results(m):
        return (
            local(hnew.at[m], hout.at[0, m], out_sem.at[m, 0]),
            local(cnew.at[m], cout.at[0, m], out_sem.at[m, 1]),
        )

    def wait_x(m):
        main, up, down = sends(m)
        main.wait_recv()
        pl.when(bottom)(up.wait_recv)
        pl.when(top)(down.wait_recv)

    def wait_h(extra):
        state_in[0].wait()
        pl.when(bottom)(h_up.wait_recv)
        pl.when(top)(h_down.wait_recv)
        if extra:
            frames_in.wait()
            pl.when(bottom)(f_up.wait_recv)
            pl.when(top)(f_down.wait_recv)

    def padded(ref, m):
        return ref[m].astype(F32)

    def row_pairs(ref, m):
        low = ref[m].astype(F32)
        high = jnp.concatenate([low[1:], jnp.zeros_like(low[:1])], axis=0)
        return lane_halves(low, high)

    def compact(src, dst, taps):
        for a in range(taps):
            for b in range(KER):
                part = [src[a, b, :, 128 * g : 128 * (g + 1)].astype(F32) for g in range(4)]
                dst[a, b, :, 0:128] = lane_halves(part[1], part[0]).astype(BF16)
                dst[a, b, :, 128:256] = lane_halves(part[3], part[2]).astype(BF16)

    def compact_bias():
        part = [bias[:, 128 * g : 128 * (g + 1)] for g in range(4)]
        lane = lax.broadcasted_iota(jnp.int32, (1, 128), 1)
        swap = lambda x: jnp.concatenate([x[:, 64:], x[:, :64]], axis=1)
        biasc[:, 0:128] = jnp.where(lane < 64, part[1], swap(part[0]))
        biasc[:, 128:256] = jnp.where(lane < 64, part[3], swap(part[2]))

    piece = 2

    def finish(m, narrow):
        for r in range(0, rows, piece):
            at = slice(r * cols, (r + piece) * cols)
            old = cell[m, r : r + piece].reshape(piece * cols, 128)
            if narrow:
                fi = sigmoid(acc[m, at, 0:128] + biasc[:, 0:128])
                og = acc[m, at, 128:256] + biasc[:, 128:256]
                gained = pltpu.roll(fi * jnp.tanh(og), 64, 1)
                new = fi * old + gained
                out = sigmoid(og) * jnp.tanh(new)
                lane = lax.broadcasted_iota(jnp.int32, new.shape, 1)
                new = jnp.where(lane < 64, new, 0.0)
                out = jnp.where(lane < 64, out, 0.0)
            else:
                gate = [acc[m, at, 128 * g : 128 * (g + 1)] + bias[:, 128 * g : 128 * (g + 1)] for g in range(4)]
                new = sigmoid(gate[1]) * old + sigmoid(gate[0]) * jnp.tanh(gate[2])
                out = sigmoid(gate[3]) * jnp.tanh(new)
            cnew[m, r : r + piece] = new.reshape(piece, cols, 128)
            hnew[m, r : r + piece] = out.astype(BF16).reshape(piece, cols, 128)

    def emit(m, layer):
        if layer < 3:
            main, up, down = sends(m)
            main.start()
            pl.when(top)(up.start)
            pl.when(bottom)(down.start)
        for copy in results(m):
            copy.start()

    def wait_small():
        state_in[1].wait()
        state_in[2].wait()

    @pl.when(seg == 0)
    def _():
        for copy in weight_copies(0):
            copy.wait()
        compact(wx, wxc, KER)
        wait_small()
        compact_bias()
        wait_h(True)

        @pl.loop(0, batches)
        def _(m):
            f = fraw[m].astype(F32)
            f = jnp.concatenate([f, jnp.zeros_like(f)], axis=-1)
            put_shifts(lane_halves(f, hraw[m].astype(F32)), shift_a)
            acc[m, :, 0:256] = conv(shift_a, wxc, rows, cols, 1)
            finish(m, True)
            emit(m, 0)

    def wide(layer, x_first):
        copies = list(weight_copies(layer))
        for copy in copies[:KER]:
            copy.wait()
        wait_h(False)

        def hidden(m):
            put_shifts(padded(hraw, m), shift_a)
            acc[m] = conv(shift_a, wh, rows, cols, 1)

        def incoming(m):
            wait_x(m)
            if layer == 1:
                put_shifts(row_pairs(xraw, m), shift_b)
                acc[m] += conv(shift_b, w3, rows, cols, 2)
            else:
                put_shifts(padded(xraw, m), shift_b)
                acc[m] += conv(shift_b, wx, rows, cols, 1)
            finish(m, False)
            emit(m, layer)

        pl.loop(0, x_first)(hidden)
        for copy in copies[KER:]:
            copy.wait()
        wait_small()

        @pl.loop(0, batches)
        def _(m):
            incoming(m)
            pl.when(m + x_first < batches)(lambda: hidden(m + x_first))

    @pl.when(seg == 1)
    def _():
        w3[2, :, 64:128] = jnp.zeros((KER, 64, 512), BF16)
        wide(1, 2)

    @pl.when(seg == 2)
    def _():
        wide(2, 3)

    @pl.when(seg == 3)
    def _():
        w3[2, :, 64:128] = jnp.zeros((KER, 64, 512), BF16)
        copies = list(weight_copies(3))
        for copy in copies[:KER]:
            copy.wait()
        compact(w3, w3c, 3)
        wait_h(False)

        @pl.loop(0, batches)
        def _(m):
            put_shifts(row_pairs(hraw, m), shift_a)
            acc[m, :, 0:256] = conv(shift_a, w3c, rows, cols, 2)

        for copy in copies[KER:]:
            copy.wait()
        compact(wx, wxc, KER)
        wait_small()
        compact_bias()

        @pl.loop(0, batches)
        def _(m):
            wait_x(m)
            put_shifts(padded(xraw, m), shift_b)
            acc[m, :, 0:256] += conv(shift_b, wxc, rows, cols, 1)
            finish(m, True)
            emit(m, 3)

    @pl.loop(0, batches)
    def _(m):
        for copy in results(m):
            copy.wait()

        @pl.when(seg < 3)
        def _():
            main, up, down = sends(m)
            main.wait_send()
            pl.when(top)(up.wait_send)
            pl.when(bottom)(down.wait_send)

    pl.when(top)(h_up.wait_send)
    pl.when(bottom)(h_down.wait_send)
    pl.when(jnp.logical_and(seg == 0, top))(f_up.wait_send)
    pl.when(jnp.logical_and(seg == 0, bottom))(f_down.wait_send)


def on_device(frames, hidden_prev, cell_prev, kernels, biases):
    segments, spaces = (lax.axis_size("segment"), lax.axis_size("space"))
    batches, rows, cols, narrow = frames.shape
    wide = hidden_prev.shape[-1]
    tall = rows + 2 * HALO
    anywhere = pl.BlockSpec(memory_space=pl.ANY)
    vmem, dma = (pltpu.VMEM, pltpu.SemaphoreType.DMA)
    return pl.pallas_call(
        functools.partial(kernel, segments, spaces),
        out_shape=(
            jax.ShapeDtypeStruct(hidden_prev.shape, BF16),
            jax.ShapeDtypeStruct(cell_prev.shape, F32),
        ),
        in_specs=[anywhere] * 5,
        out_specs=[anywhere] * 2,
        scratch_shapes=[
            vmem((KER, KER, 128, 512), BF16),
            vmem((KER, KER, 128, 512), BF16),
            vmem((3, KER, 128, 512), BF16),
            vmem((KER, KER, 128, 256), BF16),
            vmem((3, KER, 128, 256), BF16),
            vmem((1, 512), F32),
            vmem((1, 256), F32),
            vmem((batches, tall, cols, narrow), BF16),
            vmem((batches, tall, cols, wide), BF16),
            vmem((batches, tall, cols, wide), BF16),
            vmem((tall, cols, KER * wide), BF16),
            vmem((tall, cols, KER * wide), BF16),
            vmem((batches, rows * cols, 4 * wide), F32),
            vmem((batches, rows, cols, wide), F32),
            vmem((batches, rows, cols, wide), F32),
            vmem((batches, rows, cols, wide), BF16),
            dma((2 * KER,)),
            dma((4,)),
            dma((4,)),
            dma((4,)),
            dma((batches, 3)),
            dma((batches, 3)),
            dma((batches, 2)),
        ],
        compiler_params=pltpu.CompilerParams(
            collective_id=0, has_side_effects=True, vmem_limit_bytes=56 * 2**20
        ),
        name="step",
    )(frames, hidden_prev, cell_prev, kernels, biases)


def solution(mesh):
    return jax.shard_map(
        on_device,
        mesh=mesh,
        in_specs=(
            P(None, "space", None, None),
            P("segment", None, "space", None, None),
            P("segment", None, "space", None, None),
            P("segment", None, None, None, None),
            P("segment", None),
        ),
        out_specs=(
            P("segment", None, "space", None, None),
            P("segment", None, "space", None, None),
        ),
        check_vma=False,
    )
```
